32 devices in a mesh: rows: 8 (over y, x, core), sub: 4 (over z).
Axes of the slice: x: 2, y: 2, z: 4, core: 2. Of those that a mesh axis runs over, the one named last changes fastest.
Arguments:
- old_basis: bfloat16 [32, 524288], P(None, ('rows', 'sub')), may hold values from -1 to 1
- snapshots: bfloat16 [512, 524288], P(None, ('rows', 'sub')), may hold values from -16 to 16
- gap_flags: int32 [512, 4096], P(None, ('rows', 'sub')), may hold values from 0 to 1, as said below
- sketch_seed: int32 [512, 64], replicated, may hold values from -1 to 1
Outputs:
- new_basis: float32 [32, 524288], P(None, ('rows', 'sub'))
- coefficients: float32 [32, 512], replicated
The draws below stay inside these ranges and needn't reach their ends.
Inputs may be any that keep to these rules, and one draw needn't show every extreme that they name: `gap_flags`: 1 marks a block of 128 velocity rows measured in that snapshot, 0 a gap; every snapshot has measured blocks and gaps.
All inputs are finite; a program needn't handle non-finite values.
Results may differ from the reference program's by a relative error of at most 0.00135.
The reference program's roundings to bfloat16 on the way count: a program that leaves them out, or rounds other values in their place, can miss the bound.
Values may be sent and summed in bfloat16 or wider, within the bound.
No kernel may reach another device: no remote copies, remote signals or barrier semaphores. Data moves between devices by JAX's collectives and lax.ppermute only.
A program may use at most 192 MiB of HBM per device.

```python
import math
import jax
import jax.numpy as jnp
from jax import lax

K = 32
P_SIZE = 64
S = 512
BLOCK = 128
POWER = 2
R_DEV = 16384
ROWS = 524288
NBLK = 4096


def shared_basis(key):
    own_key = jax.random.fold_in(key, 7)
    common_key = jax.random.fold_in(key, 8)
    phase_key = jax.random.fold_in(key, 9)
    tilt_key = jax.random.fold_in(key, 10)
    shift_key = jax.random.fold_in(key, 14)
    position = (jnp.arange(NBLK, dtype=jnp.float32) + 0.5) / NBLK
    phases = jax.random.uniform(phase_key, (K, 2), jnp.float32, 0.0, 2.0 * math.pi)
    envelope = 0.15 * jnp.exp(0.6 * (jnp.sin(2.0 * math.pi * position[None, :] + phases[:, 0:1]) + jnp.sin(4.0 * math.pi * position[None, :] + phases[:, 1:2])))
    owner = jnp.arange(NBLK, dtype=jnp.int32) * BLOCK // R_DEV
    shift = jax.random.randint(shift_key, (), 0, K, jnp.int32)
    chosen = (owner[None, :] + shift) % K == jnp.arange(K, dtype=jnp.int32)[:, None]
    envelope = envelope * jnp.where(chosen, 2.5, 1.0)
    tilt_phase = jax.random.uniform(tilt_key, (K, 1), jnp.float32, 0.0, 2.0 * math.pi)
    frequency = (jnp.arange(K, dtype=jnp.float32) % 3.0 + 1.0)[:, None]
    tilt = jnp.cos(2.0 * math.pi * frequency * position[None, :] + tilt_phase)
    own_part = jax.random.normal(own_key, (K, NBLK, BLOCK), jnp.float32)
    common_part = jax.random.normal(common_key, (1, NBLK, BLOCK), jnp.float32)
    values = envelope[:, :, None] * (own_part + tilt[:, :, None] * common_part)
    return jnp.clip(values.reshape(K, ROWS), -1.0, 1.0)


def draw_old_basis(key, part):
    return shared_basis(key).astype(jnp.bfloat16)


def draw_snapshots(key, part):
    modes_all = shared_basis(key)
    amp_key = jax.random.fold_in(key, 11)
    noise_key = jax.random.fold_in(key, 12)
    amplitudes = jax.random.normal(amp_key, (K, S), jnp.float32) * (3.2 / math.sqrt(K))
    noise_part = jax.random.normal(noise_key, (S, ROWS), jnp.float32) * 0.6
    summed = noise_part
    for mode_index in range(K):
        summed = summed + amplitudes[mode_index][:, None] * modes_all[mode_index][None, :]
    return jnp.clip(summed, -16.0, 16.0).astype(jnp.bfloat16)


def draw_gap_flags(key, part):
    percent = jax.random.randint(jax.random.fold_in(key, 21), (S, 1), 5, 61, jnp.int32)
    run_count = jax.random.randint(jax.random.fold_in(key, 22), (S, 1), 1, 5, jnp.int32)
    run_length = NBLK * percent // (100 * run_count)
    starts = jax.random.randint(jax.random.fold_in(key, 23), (S, 4), 0, NBLK, jnp.int32)
    blocks = jnp.arange(NBLK, dtype=jnp.int32)[None, :]
    inside = jnp.zeros((S, NBLK), dtype=bool)
    for run_index in range(4):
        active = run_count > run_index
        distance = (blocks - starts[:, run_index:run_index + 1]) % NBLK
        inside = inside | active & (distance < run_length)
    return jnp.where(inside, 0, 1).astype(jnp.int32)


def with_ends(entries, key, low, top_value):
    shape = entries.shape
    index_at = [jax.random.randint(jax.random.fold_in(key, axis), (), 0, shape[axis]) for axis in range(len(shape))]
    entries = entries.at[tuple(index_at)].set(low)
    longest = shape.index(max(shape))
    index_at[longest] = (index_at[longest] + 1) % shape[longest]
    return entries.at[tuple(index_at)].set(top_value)


def setup_inputs(seed: int = 0) -> dict:
    seeds = jax.random.split(jax.random.key(seed), 5)
    old_basis = draw_old_basis(jax.random.fold_in(seeds[4], 71), 0)
    snapshots = draw_snapshots(jax.random.fold_in(seeds[4], 71), 0)
    gap_flags = draw_gap_flags(jax.random.fold_in(seeds[4], 71), 0)
    sketch_seed = with_ends(jax.random.randint(seeds[3], (S, P_SIZE), -1, 2), jax.random.fold_in(seeds[3], 1), -1, 1).astype(jnp.int32)
    return {"old_basis": old_basis, "snapshots": snapshots, "gap_flags": gap_flags, "sketch_seed": sketch_seed}


damping = 0.005
highest = lax.Precision.HIGHEST

def cholesky_last(system):
    extent = system.shape[0]
    factor = jnp.zeros_like(system)
    for column in range(extent):
        partial_sum = lax.optimization_barrier(jnp.sum(factor * factor[column:column + 1], axis=1))
        remain = system[:, column] - partial_sum
        diagonal_root = jnp.sqrt(remain[column])
        lower_part = (jnp.arange(extent) >= column).reshape((extent,) + (1,) * (system.ndim - 2))
        factor = factor.at[:, column].set(jnp.where(lower_part, remain / diagonal_root, 0.0))
    return factor

def lower_solve(factor, target):
    extent = factor.shape[0]
    result = jnp.zeros_like(target)
    for column in range(extent):
        current = (target[column] - lax.optimization_barrier(jnp.sum(factor[column] * result, axis=0))) / factor[column, column]
        result = result.at[column].set(current)
    return result

def upper_solve(factor, target):
    extent = factor.shape[0]
    result = jnp.zeros_like(target)
    for column in reversed(range(extent)):
        current = (target[column] - lax.optimization_barrier(jnp.sum(factor[:, column] * result, axis=0))) / factor[column, column]
        result = result.at[column].set(current)
    return result

def solve_normal(grams, right, modes, rows_all):
    snapshot_count = grams.shape[0]
    identity = jnp.eye(modes, dtype=jnp.float32)[:, :, None]
    system = grams.T.reshape(modes, modes, snapshot_count) + damping * rows_all * identity
    factor = cholesky_last(system)
    return upper_solve(factor, lower_solve(factor, right.T))

def inverse_factor(products):
    extent = products.shape[0]
    factor = cholesky_last(products[:, :, None])
    return lower_solve(factor, jnp.eye(extent, dtype=jnp.float32))

def mask_blocks(samples, flag_blocks):
    snapshot_count, blocks_dev = flag_blocks.shape
    weights = flag_blocks.astype(samples.dtype)[:, :, None]
    return (samples.reshape(snapshot_count, blocks_dev, -1) * weights).reshape(snapshot_count, -1)

def refill(samples, flag_blocks, recon_low):
    snapshot_count, blocks_dev = flag_blocks.shape
    observed = (flag_blocks > 0)[:, :, None]
    combined = jnp.where(observed, samples.reshape(snapshot_count, blocks_dev, -1), recon_low.reshape(snapshot_count, blocks_dev, -1))
    return combined.reshape(snapshot_count, -1)

def contract_rows(former, latter):
    return lax.dot_general(former, latter, (((1,), (1,)), ((), ())), preferred_element_type=jnp.float32)

def contract_first(former, latter):
    return lax.dot_general(former, latter, (((0,), (0,)), ((), ())), preferred_element_type=jnp.float32)

def reference(old_basis, snapshots, gap_flags, sketch_seed):
    panels = ROWS // R_DEV
    blocks_dev = R_DEV // BLOCK
    positions = jnp.arange(panels, dtype=jnp.int32)

    def panel_of(position):
        offset = position * R_DEV
        basis_part = lax.dynamic_slice_in_dim(old_basis, offset, R_DEV, 1)
        data_part = lax.dynamic_slice_in_dim(snapshots, offset, R_DEV, 1)
        flag_part = lax.dynamic_slice_in_dim(gap_flags, position * blocks_dev, blocks_dev, 1)
        return (basis_part, data_part, flag_part)

    def add_up(summand, initial):

        def accumulate(running, position):
            return (jax.tree.map(jnp.add, running, summand(position)), None)
        return lax.scan(accumulate, initial, positions)[0]

    def normal_term(position):
        basis_part, data_part, flag_part = panel_of(position)
        masked = mask_blocks(data_part, flag_part)
        right = contract_rows(masked, basis_part)
        pieces = basis_part.reshape(K, blocks_dev, BLOCK).astype(jnp.float32)
        block_grams = jnp.einsum('kbi,lbi->bkl', pieces, pieces, precision=highest)
        grams = jnp.dot(flag_part.astype(jnp.float32), block_grams.reshape(blocks_dev, K * K), precision=highest)
        return (grams, right)
    grams, right = add_up(normal_term, (jnp.zeros((S, K * K), jnp.float32), jnp.zeros((S, K), jnp.float32)))
    coefficients = solve_normal(grams, right, K, ROWS)
    coeff_low = coefficients.astype(jnp.bfloat16)

    def fill(position):
        basis_part, data_part, flag_part = panel_of(position)
        recon_low = contract_first(coeff_low, basis_part).astype(jnp.bfloat16)
        return refill(data_part, flag_part, recon_low)

    def sketch_of(position, mixer):
        return contract_first(mixer, fill(position))
    mixer = sketch_seed.astype(jnp.bfloat16)
    inverse = None
    for sweep_index in range(POWER + 1):

        def gram_term(position, mixer=mixer):
            sketch = sketch_of(position, mixer)
            return lax.dot_general(sketch, sketch, (((1,), (1,)), ((), ())), precision=highest, preferred_element_type=jnp.float32)
        products = add_up(gram_term, jnp.zeros((P_SIZE, P_SIZE), jnp.float32))
        inverse = inverse_factor(products)
        if sweep_index < POWER:

            def project_term(position, mixer=mixer, inverse=inverse):
                ortho_rows = jnp.dot(inverse, sketch_of(position, mixer), precision=highest).astype(jnp.bfloat16)
                return contract_rows(fill(position), ortho_rows)
            mixer = add_up(project_term, jnp.zeros((S, P_SIZE), jnp.float32)).astype(jnp.bfloat16)
    root_rows = math.sqrt(ROWS)

    def basis_term(position):
        return jnp.dot(inverse[:K], sketch_of(position, mixer), precision=highest) * root_rows
    stacked = lax.map(basis_term, positions)
    new_basis = jnp.transpose(stacked, (1, 0, 2)).reshape(K, ROWS)
    return (new_basis, coefficients)
```

```python
import functools
import math

import jax
import jax.numpy as jnp
from jax import lax
from jax.experimental import pallas as pl
from jax.experimental.pallas import tpu as pltpu
from jax.sharding import PartitionSpec as P

POWER = 2
DAMPING = 0.005
AXES = ("rows", "sub")
LANES = 128
HIGHEST = lax.Precision.HIGHEST
F32 = jnp.float32
BF16 = jnp.bfloat16

CONTRACT_LANES = (((1,), (1,)), ((), ()))


def dot_nt(left, right, precision=None):
    return lax.dot_general(
        left, right, CONTRACT_LANES, precision=precision, preferred_element_type=F32
    )


def dot_nn(left, right, precision=None):
    return jnp.dot(left, right, precision=precision, preferred_element_type=F32)


def split_three(values):
    first = values.astype(BF16)
    rest = values - first.astype(F32)
    second = rest.astype(BF16)
    third = (rest - second.astype(F32)).astype(BF16)
    return first, second, third


def flag_columns(flags_ref, blocks_step):
    shift = (LANES - pl.program_id(0) * blocks_step) % LANES
    return pltpu.roll(flags_ref[...].astype(F32), shift, 1).astype(BF16)


def normal_kernel(blocks_step, flags_ref, snap_ref, basis_ref, out_ref, gram_ref, right_ref):
    step = pl.program_id(0)
    count = flags_ref.shape[0]
    modes = basis_ref.shape[0]
    half = modes // 2
    columns = flag_columns(flags_ref, blocks_step)

    @pl.when(step == 0)
    def _():
        right_ref[...] = jnp.zeros_like(right_ref)

    masked = []
    for block in range(blocks_step):
        part = pl.ds(block * LANES, LANES)
        weight = jnp.broadcast_to(columns[:, block : block + 1], (count, LANES))
        masked.append(snap_ref[:, part] * weight)
        piece = basis_ref[:, part]
        copies = jnp.concatenate([piece] * (LANES // modes), axis=0)
        row = pl.multiple_of((step * blocks_step + block) * modes, modes)
        gram_ref[pl.ds(row, modes), :] = dot_nt(piece, copies)
    right_ref[...] += dot_nt(jnp.concatenate(masked, axis=1), basis_ref[...])

    @pl.when(step == pl.num_programs(0) - 1)
    def _():
        lane = lax.broadcasted_iota(jnp.int32, (LANES, LANES), 1)
        group = LANES // half
        tiles = []
        middle = jnp.zeros((LANES, LANES), F32)
        for tile_index in range(modes // group):
            tile = jnp.zeros((LANES, LANES), F32)
            for inner in range(group):
                mode = tile_index * group + inner
                rows = gram_ref[pl.ds(mode, LANES, stride=modes), :]
                moved = pltpu.roll(rows, (half * inner - mode) % LANES, 1)
                tile = jnp.where(lane // half == inner, moved, tile)
                if mode < half:
                    middle = jnp.where(lane == mode + half, rows, middle)
            tiles.append(tile)
        tiles.append(middle)
        block_rows = jnp.concatenate(tiles, axis=1)
        flags = flags_ref[...].astype(BF16)
        total = sum(dot_nn(flags, part) for part in split_three(block_rows))
        wide = tiles[0].shape[1] * (len(tiles) - 1)
        out_ref[:, :wide] = total[:, :wide]
        right = jnp.concatenate(
            [
                jnp.zeros((count, modes), F32),
                right_ref[...],
                jnp.zeros((count, LANES - 2 * modes), F32),
            ],
            axis=1,
        )
        out_ref[:, wide:] = total[:, wide:] + right


def normal_terms(flags, snapshots, basis, chunk=2048):
    count, rows = snapshots.shape
    modes = basis.shape[0]
    blocks = flags.shape[1]
    width = modes * modes // 2 + LANES
    return pl.pallas_call(
        functools.partial(normal_kernel, chunk // LANES),
        grid=(rows // chunk,),
        in_specs=[
            pl.BlockSpec((count, blocks), lambda i: (0, 0)),
            pl.BlockSpec((count, chunk), lambda i: (0, i)),
            pl.BlockSpec((modes, chunk), lambda i: (0, i)),
        ],
        out_specs=pl.BlockSpec((count, width), lambda i: (0, 0)),
        out_shape=jax.ShapeDtypeStruct((count, width), F32),
        scratch_shapes=[
            pltpu.VMEM((blocks * modes, LANES), F32),
            pltpu.VMEM((count, modes), F32),
        ],
        compiler_params=pltpu.CompilerParams(vmem_limit_bytes=48 << 20),
        name="normal_terms",
    )(flags, snapshots, basis)


def solve_kernel(modes, shift, in_ref, out_ref, turned_ref, system_ref):
    half = modes // 2
    count, width = in_ref.shape
    padded = jnp.concatenate([in_ref[...], jnp.zeros((LANES - count, width), F32)], axis=0)
    turned_ref[...] = padded.T
    for mode in range(modes):
        first = min(half, modes - mode)
        base = mode * half
        start = mode * modes + mode
        values = turned_ref[base : base + first, :]
        system_ref[start : start + first, :] = values
        if first < half:
            wrapped = turned_ref[base + first : base + half, :]
            system_ref[pl.ds(mode, half - first, stride=modes), :] = wrapped
    middle = modes * half + half
    system_ref[pl.ds(half, half, stride=modes + 1), :] = turned_ref[middle : middle + half, :]
    right = turned_ref[modes * half + modes : modes * half + 2 * modes, :]
    index = lax.broadcasted_iota(jnp.int32, (modes, LANES), 0)

    rows = [system_ref[k * modes : (k + 1) * modes, :] for k in range(modes)]
    scaled = []
    targets = []
    for column in range(modes):
        row = jnp.where(index == column, rows[column] + shift, rows[column])
        inverse = 1.0 / row[column : column + 1, :]
        factor = jnp.where(index > column, row * inverse, 0.0)
        target = right[column : column + 1, :]
        scaled.append(factor)
        targets.append(target * inverse)
        right = right - factor * target
        for k in range(column + 1, modes):
            rows[k] = rows[k] - factor[k : k + 1, :] * row
    result = jnp.zeros((modes, LANES), F32)
    for column in reversed(range(modes)):
        value = targets[column] - jnp.sum(scaled[column] * result, axis=0, keepdims=True)
        result = jnp.where(index == column, value, result)
    square = jnp.concatenate([result, jnp.zeros((LANES - modes, LANES), F32)], axis=0)
    out_ref[...] = square.T[:count, :modes]


def solve_share(share, modes, rows_all):
    count, width = share.shape
    return pl.pallas_call(
        functools.partial(solve_kernel, modes, DAMPING * rows_all),
        out_shape=jax.ShapeDtypeStruct((count, modes), F32),
        scratch_shapes=[
            pltpu.VMEM((width, LANES), F32),
            pltpu.VMEM((modes * modes, LANES), F32),
        ],
        name="solve_share",
    )(share)


def packed_blocks(tiles):
    return [(i, (i + d) % tiles) for d in range(tiles // 2) for i in range(tiles)] + [
        (i, i + tiles // 2) for i in range(tiles // 2)
    ]


def refill_kernel(
    blocks_step, flags_ref, snap_ref, basis_ref, coef_ref, fill_ref, corr_ref, sum_ref
):
    step = pl.program_id(0)
    count = flags_ref.shape[0]
    columns = flag_columns(flags_ref, blocks_step)
    coef = coef_ref[...].astype(BF16)

    @pl.when(step == 0)
    def _():
        sum_ref[...] = jnp.zeros_like(sum_ref)

    recon = dot_nn(coef, basis_ref[...]).astype(BF16)
    for block in range(blocks_step):
        part = pl.ds(block * LANES, LANES)
        weight = jnp.broadcast_to(columns[:, block : block + 1], (count, LANES))
        fill_ref[:, part] = jnp.where(
            weight > 0, snap_ref[:, part], recon[:, block * LANES : (block + 1) * LANES]
        )
    side = count // 2
    upper, lower = fill_ref[:side, :], fill_ref[side:, :]
    sum_ref[:side, :side] += dot_nt(upper, upper)
    sum_ref[:side, side:] += dot_nt(upper, lower)
    sum_ref[side:, side:] += dot_nt(lower, lower)

    @pl.when(step == pl.num_programs(0) - 1)
    def _():
        for place, (i, j) in enumerate(packed_blocks(count // LANES)):
            i, j = min(i, j), max(i, j)
            corr_ref[place * LANES : (place + 1) * LANES, :] = sum_ref[
                i * LANES : (i + 1) * LANES, j * LANES : (j + 1) * LANES
            ]


def refill_correlate(flags, snapshots, basis, coefs, chunk=2048):
    count, rows = snapshots.shape
    modes = basis.shape[0]
    blocks = flags.shape[1]
    packed = len(packed_blocks(count // LANES)) * LANES
    return pl.pallas_call(
        functools.partial(refill_kernel, chunk // LANES),
        grid=(rows // chunk,),
        in_specs=[
            pl.BlockSpec((count, blocks), lambda i: (0, 0)),
            pl.BlockSpec((count, chunk), lambda i: (0, i)),
            pl.BlockSpec((modes, chunk), lambda i: (0, i)),
            pl.BlockSpec((count, modes), lambda i: (0, 0)),
        ],
        out_specs=[
            pl.BlockSpec((count, chunk), lambda i: (0, i)),
            pl.BlockSpec((packed, LANES), lambda i: (0, 0)),
        ],
        out_shape=[
            jax.ShapeDtypeStruct((count, rows), BF16),
            jax.ShapeDtypeStruct((packed, LANES), F32),
        ],
        scratch_shapes=[pltpu.VMEM((count, count), F32)],
        compiler_params=pltpu.CompilerParams(vmem_limit_bytes=48 << 20),
        name="refill_correlate",
    )(flags, snapshots, basis, coefs)


def inverse_cholesky(products):
    extent = products.shape[0]
    row_index = lax.broadcasted_iota(jnp.int32, (extent, 2 * extent), 0)
    lane_index = lax.broadcasted_iota(jnp.int32, (extent, 2 * extent), 1)
    eye = jnp.where(
        lax.broadcasted_iota(jnp.int32, (extent, extent), 0)
        == lax.broadcasted_iota(jnp.int32, (extent, extent), 1),
        1.0,
        0.0,
    )
    work = jnp.concatenate([products, eye], axis=1)
    for column in range(extent - 1):
        row = work[column : column + 1, :]
        factor = work[:, column : column + 1] / row[:, column : column + 1]
        factor = jnp.broadcast_to(factor, work.shape)
        work = work - jnp.where(row_index > column, factor * row, 0.0)
    pivots = jnp.sum(jnp.where(row_index == lane_index, work, 0.0), axis=1, keepdims=True)
    return work[:, extent:] * (1.0 / jnp.sqrt(pivots))


def sweep_weights(mixer, full, rows):
    spread = dot_nn(mixer, full, HIGHEST)
    products = dot_nt(spread, mixer, HIGHEST)
    return dot_nn(inverse_cholesky(products)[:rows], mixer, HIGHEST)


def first_kernel(corr_ref, seed_ref, out_ref, full_ref):
    count = full_ref.shape[0]
    for place, (i, j) in enumerate(packed_blocks(count // LANES)):
        i, j = min(i, j), max(i, j)
        tile = corr_ref[place * LANES : (place + 1) * LANES, :]
        rows, cols = pl.ds(i * LANES, LANES), pl.ds(j * LANES, LANES)
        full_ref[rows, cols] = tile
        if i != j:
            full_ref[cols, rows] = tile.T
    mixer = seed_ref[...].astype(F32).T
    store_parts(out_ref, sweep_weights(mixer, full_ref[...], mixer.shape[0]))


def later_kernel(scale, full_ref, mixer_ref, out_ref):
    mixer = mixer_ref[...].astype(BF16).astype(F32)
    store_parts(out_ref, sweep_weights(mixer, full_ref[...], out_ref.shape[0] // 3) * scale)


def store_parts(out_ref, values):
    rows = values.shape[0]
    for place, part in enumerate(split_three(values)):
        out_ref[place * rows : (place + 1) * rows, :] = part


def first_weights(corr, seed):
    count, width = seed.shape
    return pl.pallas_call(
        first_kernel,
        out_shape=[
            jax.ShapeDtypeStruct((3 * width, count), BF16),
            jax.ShapeDtypeStruct((count, count), F32),
        ],
        name="first_weights",
    )(corr, seed)


def later_weights(full, mixer, rows, scale):
    return pl.pallas_call(
        functools.partial(later_kernel, scale),
        out_shape=jax.ShapeDtypeStruct((3 * rows, mixer.shape[1]), BF16),
        name="later_weights",
    )(full, mixer)


def mixer_kernel(weights_ref, fill_ref, out_ref):
    width = out_ref.shape[0]

    @pl.when(pl.program_id(0) == 0)
    def _():
        out_ref[...] = jnp.zeros_like(out_ref)

    terms = dot_nn(weights_ref[...], fill_ref[...])
    ortho = terms[:width] + (terms[width : 2 * width] + terms[2 * width :])
    out_ref[...] += dot_nt(ortho.astype(BF16), fill_ref[...])


def next_mixer(weights, filled, chunk=2048):
    count, rows = filled.shape
    width = weights.shape[0] // 3
    return pl.pallas_call(
        mixer_kernel,
        grid=(rows // chunk,),
        in_specs=[
            pl.BlockSpec(weights.shape, lambda i: (0, 0)),
            pl.BlockSpec((count, chunk), lambda i: (0, i)),
        ],
        out_specs=pl.BlockSpec((width, count), lambda i: (0, 0)),
        out_shape=jax.ShapeDtypeStruct((width, count), F32),
        compiler_params=pltpu.CompilerParams(vmem_limit_bytes=48 << 20),
        name="next_mixer",
    )(weights, filled)


def basis_kernel(weights_ref, fill_ref, out_ref):
    modes = out_ref.shape[0]
    terms = dot_nn(weights_ref[...], fill_ref[...])
    out_ref[...] = terms[:modes] + (terms[modes : 2 * modes] + terms[2 * modes :])


def project_basis(weights, filled, chunk=2048):
    count, rows = filled.shape
    modes = weights.shape[0] // 3
    return pl.pallas_call(
        basis_kernel,
        grid=(rows // chunk,),
        in_specs=[
            pl.BlockSpec(weights.shape, lambda i: (0, 0)),
            pl.BlockSpec((count, chunk), lambda i: (0, i)),
        ],
        out_specs=pl.BlockSpec((modes, chunk), lambda i: (0, i)),
        out_shape=jax.ShapeDtypeStruct((modes, rows), F32),
        compiler_params=pltpu.CompilerParams(vmem_limit_bytes=48 << 20),
        name="project_basis",
    )(weights, filled)


class Stage:
    def __init__(self, axis, size, bits):
        self.axis = axis
        self.pairs = [(i, i ^ (1 << bits[i & 1])) for i in range(size)]
        self.bits = bits

    def bit(self):
        place = lax.axis_index(self.axis)
        if self.bits[0] == self.bits[1]:
            return (place >> self.bits[0]) & 1
        return jnp.where(place & 1, place >> self.bits[1], place >> self.bits[0]) & 1

    def swap(self, values):
        return lax.ppermute(values, self.axis, self.pairs)


def stages():
    rows, sub = (lax.axis_size(name) for name in AXES)
    high = list(range(1, rows.bit_length() - 1))
    plan = [Stage("rows", rows, (0, 0))]
    plan += [Stage("rows", rows, bits) for bits in zip(high, reversed(high))]
    plan += [Stage("sub", sub, (bit, bit)) for bit in range(sub.bit_length() - 1)]
    return plan


def halve(values, stage):
    bit = stage.bit()
    half = values.shape[0] // 2
    keep = lax.dynamic_slice_in_dim(values, bit * half, half, 0)
    send = lax.dynamic_slice_in_dim(values, (1 - bit) * half, half, 0)
    return keep + stage.swap(send)


def join(values, stage):
    other = stage.swap(values)
    low = stage.bit() == 0
    return jnp.concatenate(
        [jnp.where(low, values, other), jnp.where(low, other, values)], axis=0
    )


def scatter_sum(values):
    for stage in stages():
        values = halve(values, stage)
    return values


def gather_shares(share):
    rows, sub = (lax.axis_size(name) for name in AXES)
    total = rows * sub
    spread = jnp.broadcast_to(share[None], (total, *share.shape))
    spread = lax.all_to_all(spread, AXES, 0, 0, tiled=True)
    high = rows.bit_length() - 2
    low = sub.bit_length() - 1
    cube = spread.reshape((2,) * high + (2,) + (2,) * low + share.shape)
    tail = high + low
    subs = [high + low - 1 - k for k in range(low)]
    sides = []
    for core in range(2):
        side = lax.index_in_dim(cube, core, high, keepdims=False)
        order = list(range(high)) if core else list(reversed(range(high)))
        sides.append(side.transpose(order + subs + [tail, tail + 1]))
    return jnp.stack(sides).reshape(total * share.shape[0], share.shape[1])


def sum_everywhere(values, halvings):
    plan = stages()
    for stage in plan[:halvings]:
        values = halve(values, stage)
    for stage in plan[halvings:]:
        values = values + stage.swap(values)
    for stage in reversed(plan[:halvings]):
        values = join(values, stage)
    return values


def per_device(old_basis, snapshots, gap_flags, sketch_seed):
    modes = old_basis.shape[0]
    rows_all = old_basis.shape[1] * lax.axis_size(AXES)
    terms = normal_terms(gap_flags, snapshots, old_basis)
    share = solve_share(scatter_sum(terms), modes, rows_all)
    coefs = gather_shares(share)
    filled, corr = refill_correlate(gap_flags, snapshots, old_basis, coefs)
    weights, full = first_weights(sum_everywhere(corr, 2), sketch_seed)
    width = sketch_seed.shape[1]
    for sweep in range(1, POWER + 1):
        mixer = sum_everywhere(next_mixer(weights, filled), 1)
        last = sweep == POWER
        rows = modes if last else width
        weights = later_weights(full, mixer, rows, math.sqrt(rows_all) if last else 1.0)
    return project_basis(weights, filled), coefs.T


def solution(mesh):
    split = P(None, AXES)
    return jax.shard_map(
        per_device,
        mesh=mesh,
        in_specs=(split, split, split, P()),
        out_specs=(split, P()),
        check_vma=False,
    )
```

```python
import functools
import math

import jax
import jax.numpy as jnp
from jax import lax
from jax.experimental import pallas as pl
from jax.experimental.pallas import tpu as pltpu
from jax.sharding import PartitionSpec as P

POWER = 2
DAMPING = 0.005
AXES = ("rows", "sub")
LANES = 128
SUBLANES = 8
SCRATCH_BYTES = 48 << 20
HIGHEST = lax.Precision.HIGHEST
F32 = jnp.float32
BF16 = jnp.bfloat16

CONTRACT_LANES = (((1,), (1,)), ((), ()))


def dot_nt(left, right, precision=None):
    return lax.dot_general(
        left, right, CONTRACT_LANES, precision=precision, preferred_element_type=F32
    )


def dot_nn(left, right, precision=None):
    return jnp.dot(left, right, precision=precision, preferred_element_type=F32)


def split_three(values):
    first = values.astype(BF16)
    rest = values - first.astype(F32)
    second = rest.astype(BF16)
    third = (rest - second.astype(F32)).astype(BF16)
    return first, second, third


def chunk_copy(source, target, arrived, step, chunk):
    part = chunk_at(step, chunk)
    return pltpu.make_async_copy(source.at[:, part], target.at[:, part], arrived.at[step])


def fetch_all(source, target, arrived, chunk):
    for step in range(target.shape[1] // chunk):
        chunk_copy(source, target, arrived, step, chunk).start()


def flag_columns(flags, step, blocks_step):
    shift = lax.rem(LANES - step * blocks_step, LANES)
    return pltpu.roll(flags, shift, 1).astype(BF16)


def chunk_at(step, chunk):
    return pl.ds(pl.multiple_of(step * chunk, chunk), chunk)


def normal_kernel(
    chunk,
    flags_ref,
    snap_hbm,
    basis_ref,
    out_ref,
    masked_hbm,
    snap_ref,
    masked_ref,
    gram_ref,
    right_ref,
    arrived,
    left,
):
    count, rows = snap_ref.shape
    modes = basis_ref.shape[0]
    half = modes // 2
    blocks_step = chunk // LANES
    steps = rows // chunk

    fetch_all(snap_hbm, snap_ref, arrived, chunk)
    right_ref[...] = jnp.zeros_like(right_ref)
    all_flags = flags_ref[...].astype(F32)

    for block in range(rows // LANES):
        piece = basis_ref[:, block * LANES : (block + 1) * LANES]
        copies = jnp.concatenate([piece] * (LANES // modes), axis=0)
        gram_ref[block * modes : (block + 1) * modes, :] = dot_nt(piece, copies)

    def body(step, carry):
        chunk_copy(snap_hbm, snap_ref, arrived, step, chunk).wait()
        columns = flag_columns(all_flags, step, blocks_step)
        here = chunk_at(step, chunk)
        source, target = snap_ref.at[:, here], masked_ref.at[:, here]
        for block in range(blocks_step):
            part = pl.ds(block * LANES, LANES)
            weight = jnp.broadcast_to(columns[:, block : block + 1], (count, LANES))
            target[:, part] = source[:, part] * weight
        chunk_copy(masked_ref, masked_hbm, left, step, chunk).start()
        right_ref[...] += dot_nt(target[...], basis_ref[:, here])
        return carry

    def drain(step, carry):
        chunk_copy(masked_ref, masked_hbm, left, step, chunk).wait()
        return carry

    lax.fori_loop(0, steps, body, 0)

    lane = lax.broadcasted_iota(jnp.int32, (LANES, LANES), 1)
    group = LANES // half
    tiles = []
    middle = jnp.zeros((LANES, LANES), F32)
    for tile_index in range(modes // group):
        tile = jnp.zeros((LANES, LANES), F32)
        for inner in range(group):
            mode = tile_index * group + inner
            entries = gram_ref[pl.ds(mode, LANES, stride=modes), :]
            moved = pltpu.roll(entries, (half * inner - mode) % LANES, 1)
            tile = jnp.where(lane // half == inner, moved, tile)
            if mode < half:
                middle = jnp.where(lane == mode + half, entries, middle)
        tiles.append(tile)
    tiles.append(middle)
    flags = flags_ref[...].astype(BF16)
    total = sum(
        dot_nn(flags, part) for part in split_three(jnp.concatenate(tiles, axis=1))
    )
    wide = LANES * (len(tiles) - 1)
    out_ref[:, :wide] = total[:, :wide]
    right = jnp.concatenate(
        [
            jnp.zeros((count, modes), F32),
            right_ref[...],
            jnp.zeros((count, LANES - 2 * modes), F32),
        ],
        axis=1,
    )
    out_ref[:, wide:] = total[:, wide:] + right
    lax.fori_loop(0, steps, drain, 0)


def normal_terms(flags, snapshots, basis, chunk=4096):
    count, rows = snapshots.shape
    modes = basis.shape[0]
    blocks = flags.shape[1]
    width = modes * modes // 2 + LANES
    whole = pl.BlockSpec(memory_space=pltpu.VMEM)
    return pl.pallas_call(
        functools.partial(normal_kernel, chunk),
        in_specs=[whole, pl.BlockSpec(memory_space=pl.ANY), whole],
        out_specs=[whole, pl.BlockSpec(memory_space=pl.ANY)],
        out_shape=[
            jax.ShapeDtypeStruct((count, width), F32),
            jax.ShapeDtypeStruct((count, rows), BF16),
        ],
        scratch_shapes=[
            pltpu.VMEM((count, rows), BF16),
            pltpu.VMEM((count, rows), BF16),
            pltpu.VMEM((blocks * modes, LANES), F32),
            pltpu.VMEM((count, modes), F32),
            pltpu.SemaphoreType.DMA((rows // chunk,)),
            pltpu.SemaphoreType.DMA((rows // chunk,)),
        ],
        compiler_params=pltpu.CompilerParams(vmem_limit_bytes=SCRATCH_BYTES),
        name="normal_terms",
    )(flags, snapshots, basis)


def solve_kernel(modes, shift, in_ref, out_ref, turned_ref, system_ref):
    half = modes // 2
    count, width = in_ref.shape
    padded = jnp.concatenate([in_ref[...], jnp.zeros((LANES - count, width), F32)], axis=0)
    turned_ref[...] = padded.T
    for mode in range(modes):
        first = min(half, modes - mode)
        base = mode * half
        start = mode * modes + mode
        values = turned_ref[base : base + first, :]
        system_ref[start : start + first, :] = values
        if first < half:
            wrapped = turned_ref[base + first : base + half, :]
            system_ref[pl.ds(mode, half - first, stride=modes), :] = wrapped
    middle = modes * half + half
    system_ref[pl.ds(half, half, stride=modes + 1), :] = turned_ref[middle : middle + half, :]
    right = turned_ref[modes * half + modes : modes * half + 2 * modes, :]
    index = lax.broadcasted_iota(jnp.int32, (modes, LANES), 0)

    rows = [system_ref[k * modes : (k + 1) * modes, :] for k in range(modes)]
    scaled = []
    targets = []
    for column in range(modes):
        row = jnp.where(index == column, rows[column] + shift, rows[column])
        inverse = 1.0 / row[column : column + 1, :]
        factor = jnp.where(index > column, row * inverse, 0.0)
        target = right[column : column + 1, :]
        scaled.append(factor)
        targets.append(target * inverse)
        right = right - factor * target
        for k in range(column + 1, modes):
            rows[k] = rows[k] - factor[k : k + 1, :] * row
    result = jnp.zeros((modes, LANES), F32)
    for column in reversed(range(modes)):
        value = targets[column] - jnp.sum(scaled[column] * result, axis=0, keepdims=True)
        result = jnp.where(index == column, value, result)
    square = jnp.concatenate([result, jnp.zeros((LANES - modes, LANES), F32)], axis=0)
    share = square.T[:count, :modes]
    high = out_ref.shape[1]
    dense = jnp.concatenate(
        [share[top : top + high, :] for top in range(0, count, high)], axis=1
    )
    for device in range(out_ref.shape[0]):
        out_ref[device] = dense


def solve_share(share, modes, rows_all, devices):
    count, width = share.shape
    return pl.pallas_call(
        functools.partial(solve_kernel, modes, DAMPING * rows_all),
        out_shape=jax.ShapeDtypeStruct((devices, count * modes // LANES, LANES), F32),
        scratch_shapes=[
            pltpu.VMEM((width, LANES), F32),
            pltpu.VMEM((modes * modes, LANES), F32),
        ],
        name="solve_share",
    )(share)


def packed_blocks(tiles):
    return [(i, (i + d) % tiles) for d in range(tiles // 2) for i in range(tiles)] + [
        (i, i + tiles // 2) for i in range(tiles // 2)
    ]


def refill_kernel(
    chunk,
    order,
    flags_ref,
    masked_hbm,
    basis_ref,
    shares_ref,
    fill_hbm,
    corr_ref,
    turned_ref,
    masked_ref,
    coef_ref,
    fill_ref,
    gap_ref,
    square_ref,
    sum_ref,
    arrived,
    left,
):
    count, rows = fill_ref.shape
    modes = basis_ref.shape[0]
    blocks = flags_ref.shape[1]
    group = square_ref.shape[1] // modes
    steps = rows // chunk
    side = count // 2
    fetch_all(masked_hbm, masked_ref, arrived, chunk)
    sum_ref[...] = jnp.zeros_like(sum_ref)
    square_ref[...] = jnp.zeros_like(square_ref)

    devices, high, _ = shares_ref.shape
    share_rows = count // devices
    for device in range(devices):
        dense = shares_ref[device]
        for place in range(share_rows // high):
            top = order[device] * share_rows + place * high
            coef_ref[top : top + high, :] = dense[:, place * modes : (place + 1) * modes]
    turned_ref[...] = coef_ref[...].T

    gaps = (1 - flags_ref[...]).astype(F32).astype(BF16)
    coef = coef_ref[...].astype(BF16).astype(F32)
    wide = jnp.concatenate([coef] * (2 * LANES // modes), axis=1)
    place = lax.broadcasted_iota(jnp.int32, (blocks, 2 * LANES), 0)
    owner = lax.broadcasted_iota(jnp.int32, (blocks, 2 * LANES), 1) // modes
    for part in range(blocks * modes // (2 * LANES)):
        first = part * (2 * LANES // modes)
        pick = jnp.where(place == owner + first, 1.0, 0.0).astype(BF16)
        gap_ref[:, part * 2 * LANES : (part + 1) * 2 * LANES] = (
            dot_nn(gaps, pick) * wide
        ).astype(BF16)

    def body(step, carry):
        here = chunk_at(step, chunk)
        chunk_copy(masked_hbm, masked_ref, arrived, step, chunk).wait()
        basis = basis_ref.at[:, here]
        masked, filled = masked_ref.at[:, here], fill_ref.at[:, here]
        weights = gap_ref.at[:, chunk_at(step, chunk // LANES * modes)]
        span = group * LANES
        for part in range(chunk // span):
            square = square_ref.at[part]
            for inner in range(group):
                square[
                    inner * modes : (inner + 1) * modes, inner * LANES : (inner + 1) * LANES
                ] = basis[:, part * span + inner * LANES : part * span + (inner + 1) * LANES]
            own = weights[:, part * group * modes : (part + 1) * group * modes]
            recon = dot_nn(own, square[...]).astype(BF16)
            lanes = pl.ds(part * span, span)
            filled[:, lanes] = masked[:, lanes] + recon
        chunk_copy(fill_ref, fill_hbm, left, step, chunk).start()
        upper, lower = filled[:side, :], filled[side:, :]
        sum_ref[:side, :side] += dot_nt(upper, upper)
        sum_ref[:side, side:] += dot_nt(upper, lower)
        sum_ref[side:, side:] += dot_nt(lower, lower)
        return carry

    def drain(step, carry):
        chunk_copy(fill_ref, fill_hbm, left, step, chunk).wait()
        return carry

    lax.fori_loop(0, steps, body, 0)
    for place, (i, j) in enumerate(packed_blocks(count // LANES)):
        i, j = min(i, j), max(i, j)
        corr_ref[place * LANES : (place + 1) * LANES, :] = sum_ref[
            i * LANES : (i + 1) * LANES, j * LANES : (j + 1) * LANES
        ]
    lax.fori_loop(0, steps, drain, 0)


def refill_correlate(flags, masked, basis, shares, order, chunk=4096, group=8):
    count, rows = masked.shape
    modes = basis.shape[0]
    packed = len(packed_blocks(count // LANES)) * LANES
    whole = pl.BlockSpec(memory_space=pltpu.VMEM)
    hbm = pl.BlockSpec(memory_space=pl.ANY)
    return pl.pallas_call(
        functools.partial(refill_kernel, chunk, order),
        in_specs=[whole, hbm, whole, whole],
        out_specs=[hbm, whole, whole],
        out_shape=[
            jax.ShapeDtypeStruct((count, rows), BF16),
            jax.ShapeDtypeStruct((packed, LANES), F32),
            jax.ShapeDtypeStruct((modes, count), F32),
        ],
        scratch_shapes=[
            pltpu.VMEM((count, rows), BF16),
            pltpu.VMEM((count, modes), F32),
            pltpu.VMEM((count, rows), BF16),
            pltpu.VMEM((count, flags.shape[1] * modes), BF16),
            pltpu.VMEM((chunk // (group * LANES), group * modes, group * LANES), BF16),
            pltpu.VMEM((count, count), F32),
            pltpu.SemaphoreType.DMA((rows // chunk,)),
            pltpu.SemaphoreType.DMA((rows // chunk,)),
        ],
        compiler_params=pltpu.CompilerParams(vmem_limit_bytes=SCRATCH_BYTES),
        name="refill_correlate",
    )(flags, masked, basis, shares)


def inverse_cholesky(products, panel=4):
    extent = products.shape[0]
    shape = (SUBLANES, 2 * extent)
    sub = lax.broadcasted_iota(jnp.int32, shape, 0)
    lane = lax.broadcasted_iota(jnp.int32, shape, 1)
    tiles = []
    for top in range(0, extent, SUBLANES):
        left = products[top : top + SUBLANES, :]
        both = jnp.concatenate([left, jnp.zeros_like(left)], axis=1)
        tiles.append(jnp.where(lane == sub + top + extent, 1.0, both))
    pivots = [jnp.ones(shape, F32) for _ in tiles]
    for start in range(0, extent, panel):
        first = start // SUBLANES
        inside = range(start, start + panel)
        spread = {
            (column, t): jnp.broadcast_to(tiles[t][:, column : column + 1], shape)
            for column in inside
            for t in range(first, len(tiles))
        }
        for column in inside:
            home, place = divmod(column, SUBLANES)
            pivot = spread[column, home][place : place + 1, :]
            inverse = 1.0 / pivot
            pivots[home] = jnp.where(sub == place, pivot, pivots[home])
            row = tiles[home][place : place + 1, :] * inverse
            later = range(column + 1, start + panel)
            values = {c: spread[c, home][place : place + 1, :] * inverse for c in later}
            for t in range(home, len(tiles)):
                factor = spread[column, t]
                if t == home:
                    factor = jnp.where(sub > place, factor, 0.0)
                for c in later:
                    spread[c, t] = spread[c, t] - factor * values[c]
                tiles[t] = tiles[t] - factor * row
    scaled = [tile / jnp.sqrt(pivot) for tile, pivot in zip(tiles, pivots)]
    return jnp.concatenate(scaled, axis=0)[:, extent:]


def sweep_weights(mixer, full, rows):
    spread = dot_nn(mixer, full, HIGHEST)
    products = dot_nt(spread, mixer, HIGHEST)
    return dot_nn(inverse_cholesky(products)[:rows], mixer, HIGHEST)


def first_kernel(bit_ref, mine_ref, other_ref, seed_ref, out_ref, full_ref):
    count = full_ref.shape[0]
    corr = joined(bit_ref, mine_ref, other_ref)
    for place, (i, j) in enumerate(packed_blocks(count // LANES)):
        i, j = min(i, j), max(i, j)
        tile = corr[place * LANES : (place + 1) * LANES, :]
        rows, cols = pl.ds(i * LANES, LANES), pl.ds(j * LANES, LANES)
        full_ref[rows, cols] = tile
        if i != j:
            full_ref[cols, rows] = tile.T
    mixer = seed_ref[...].astype(F32).T
    store_parts(out_ref, sweep_weights(mixer, full_ref[...], mixer.shape[0]))


def later_kernel(rows, scale, bit_ref, mine_ref, other_ref, full_ref, out_ref):
    mixer = joined(bit_ref, mine_ref, other_ref).astype(BF16).astype(F32)
    store_parts(out_ref, sweep_weights(mixer, full_ref[...], rows) * scale)


def store_parts(out_ref, values):
    rows = values.shape[0]
    for place, part in enumerate(split_three(values)):
        out_ref[place * rows : (place + 1) * rows, :] = part


def joined(bit_ref, mine_ref, other_ref):
    low = bit_ref[0] == 0
    mine, other = mine_ref[...], other_ref[...]
    return jnp.concatenate(
        [jnp.where(low, mine, other), jnp.where(low, other, mine)], axis=0
    )


def weight_specs(halves):
    scalar = pl.BlockSpec(memory_space=pltpu.SMEM)
    return [scalar] + [pl.BlockSpec(memory_space=pltpu.VMEM)] * halves


def first_weights(halves, seed):
    count, width = seed.shape
    return pl.pallas_call(
        first_kernel,
        in_specs=weight_specs(3),
        out_shape=[
            pltpu.VMEM((3 * width, count), BF16),
            pltpu.VMEM((count, count), F32),
        ],
        name="first_weights",
    )(*halves, seed)


def later_weights(halves, full, rows, scale):
    return pl.pallas_call(
        functools.partial(later_kernel, rows, scale),
        in_specs=weight_specs(3),
        out_shape=pltpu.VMEM((3 * rows, full.shape[0]), BF16),
        name="later_weights",
    )(*halves, full)


def mixer_kernel(chunk, weights_ref, fill_hbm, out_ref, fill_ref, sum_ref, arrived):
    width = out_ref.shape[0]
    fetch_all(fill_hbm, fill_ref, arrived, chunk)
    sum_ref[...] = jnp.zeros_like(sum_ref)

    def body(step, carry):
        chunk_copy(fill_hbm, fill_ref, arrived, step, chunk).wait()
        filled = fill_ref[:, chunk_at(step, chunk)]
        terms = dot_nn(weights_ref[...], filled)
        ortho = terms[:width] + (terms[width : 2 * width] + terms[2 * width :])
        sum_ref[...] += dot_nt(filled, ortho.astype(BF16))
        return carry

    lax.fori_loop(0, fill_ref.shape[1] // chunk, body, 0)
    out_ref[...] = sum_ref[...].T


def next_mixer(weights, filled, chunk=4096):
    count, rows = filled.shape
    width = weights.shape[0] // 3
    whole = pl.BlockSpec(memory_space=pltpu.VMEM)
    return pl.pallas_call(
        functools.partial(mixer_kernel, chunk),
        in_specs=[whole, pl.BlockSpec(memory_space=pl.ANY)],
        out_specs=whole,
        out_shape=jax.ShapeDtypeStruct((width, count), F32),
        scratch_shapes=[
            pltpu.VMEM((count, rows), BF16),
            pltpu.VMEM((count, width), F32),
            pltpu.SemaphoreType.DMA((rows // chunk,)),
        ],
        compiler_params=pltpu.CompilerParams(vmem_limit_bytes=SCRATCH_BYTES),
        name="next_mixer",
    )(weights, filled)


def basis_kernel(chunk, weights_ref, fill_hbm, out_hbm, fill_ref, out_ref, arrived, left):
    modes, rows = out_ref.shape
    fetch_all(fill_hbm, fill_ref, arrived, chunk)

    def body(step, carry):
        here = chunk_at(step, chunk)
        chunk_copy(fill_hbm, fill_ref, arrived, step, chunk).wait()
        terms = dot_nn(weights_ref[...], fill_ref[:, here])
        out_ref[:, here] = terms[:modes] + (terms[modes : 2 * modes] + terms[2 * modes :])
        chunk_copy(out_ref, out_hbm, left, step, chunk).start()
        return carry

    def drain(step, carry):
        chunk_copy(out_ref, out_hbm, left, step, chunk).wait()
        return carry

    lax.fori_loop(0, rows // chunk, body, 0)
    lax.fori_loop(0, rows // chunk, drain, 0)


def project_basis(weights, filled, chunk=4096):
    count, rows = filled.shape
    modes = weights.shape[0] // 3
    hbm = pl.BlockSpec(memory_space=pl.ANY)
    return pl.pallas_call(
        functools.partial(basis_kernel, chunk),
        in_specs=[pl.BlockSpec(memory_space=pltpu.VMEM), hbm],
        out_specs=hbm,
        out_shape=jax.ShapeDtypeStruct((modes, rows), F32),
        scratch_shapes=[
            pltpu.VMEM((count, rows), BF16),
            pltpu.VMEM((modes, rows), F32),
            pltpu.SemaphoreType.DMA((rows // chunk,)),
            pltpu.SemaphoreType.DMA((rows // chunk,)),
        ],
        compiler_params=pltpu.CompilerParams(vmem_limit_bytes=SCRATCH_BYTES),
        name="project_basis",
    )(weights, filled)


class Stage:
    def __init__(self, axis, size, bits):
        self.axis = axis
        self.pairs = [(i, i ^ (1 << bits[i & 1])) for i in range(size)]
        self.bits = bits

    def bit(self):
        place = lax.axis_index(self.axis)
        if self.bits[0] == self.bits[1]:
            return (place >> self.bits[0]) & 1
        return jnp.where(place & 1, place >> self.bits[1], place >> self.bits[0]) & 1

    def swap(self, values):
        return lax.ppermute(values, self.axis, self.pairs)


def stages():
    rows, sub = (lax.axis_size(name) for name in AXES)
    high = list(range(1, rows.bit_length() - 1))
    plan = [Stage("rows", rows, (0, 0))]
    plan += [Stage("rows", rows, bits) for bits in zip(high, reversed(high))]
    plan += [Stage("sub", sub, (bit, bit)) for bit in range(sub.bit_length() - 1)]
    return plan


def halve(values, stage):
    bit = stage.bit()
    half = values.shape[0] // 2
    keep = lax.dynamic_slice_in_dim(values, bit * half, half, 0)
    send = lax.dynamic_slice_in_dim(values, (1 - bit) * half, half, 0)
    return keep + stage.swap(send)


def join(values, stage):
    other = stage.swap(values)
    low = stage.bit() == 0
    return jnp.concatenate(
        [jnp.where(low, values, other), jnp.where(low, other, values)], axis=0
    )


def scatter_sum(values):
    for stage in stages():
        values = halve(values, stage)
    return values


def share_order():
    rows, sub = (lax.axis_size(name) for name in AXES)
    order = []
    for row in range(rows):
        for column in range(sub):
            place = 0
            for stage in stages():
                index = row if stage.axis == "rows" else column
                place = 2 * place + ((index >> stage.bits[row & 1]) & 1)
            order.append(place)
    return order


def sum_everywhere(values, halvings):
    plan = stages()
    for stage in plan[:halvings]:
        values = halve(values, stage)
    for stage in plan[halvings:]:
        values = values + stage.swap(values)
    for stage in reversed(plan[1:halvings]):
        values = join(values, stage)
    core = plan[0]
    return core.bit().astype(jnp.int32).reshape(1), values, core.swap(values)


def per_device(old_basis, snapshots, gap_flags, sketch_seed):
    modes = old_basis.shape[0]
    rows_all = old_basis.shape[1] * lax.axis_size(AXES)
    terms, masked = normal_terms(gap_flags, snapshots, old_basis)
    devices = lax.axis_size(AXES)
    shares = solve_share(scatter_sum(terms), modes, rows_all, devices)
    shares = lax.all_to_all(shares, AXES, 0, 0, tiled=True)
    filled, corr, coefs = refill_correlate(gap_flags, masked, old_basis, shares, share_order())
    weights, full = first_weights(sum_everywhere(corr, 2), sketch_seed)
    width = sketch_seed.shape[1]
    for sweep in range(1, POWER + 1):
        halves = sum_everywhere(next_mixer(weights, filled), 1)
        if sweep < POWER:
            weights = later_weights(halves, full, width, 1.0)
        else:
            weights = later_weights(halves, full, modes, math.sqrt(rows_all))
    return project_basis(weights, filled), coefs


def solution(mesh):
    split = P(None, AXES)
    return jax.shard_map(
        per_device,
        mesh=mesh,
        in_specs=(split, split, split, P()),
        out_specs=(split, P()),
        check_vma=False,
    )
```

```python
import functools
import math

import jax
import jax.numpy as jnp
from jax import lax
from jax.experimental import pallas as pl
from jax.experimental.pallas import tpu as pltpu
from jax.sharding import PartitionSpec as P

POWER = 2
DAMPING = 0.005
AXES = ("rows", "sub")
LANES = 128
SUBLANES = 8
SCRATCH_BYTES = 48 << 20
HIGHEST = lax.Precision.HIGHEST
F32 = jnp.float32
BF16 = jnp.bfloat16

CONTRACT_LANES = (((1,), (1,)), ((), ()))


def dot_nt(left, right, precision=None):
    return lax.dot_general(
        left, right, CONTRACT_LANES, precision=precision, preferred_element_type=F32
    )


def dot_nn(left, right, precision=None):
    return jnp.dot(left, right, precision=precision, preferred_element_type=F32)


def split_three(values):
    first = values.astype(BF16)
    rest = values - first.astype(F32)
    second = rest.astype(BF16)
    third = (rest - second.astype(F32)).astype(BF16)
    return first, second, third


def chunk_copy(source, target, arrived, step, chunk):
    part = chunk_at(step, chunk)
    return pltpu.make_async_copy(source.at[:, part], target.at[:, part], arrived.at[step])


def fetch_all(source, target, arrived, chunk):
    for step in range(target.shape[1] // chunk):
        chunk_copy(source, target, arrived, step, chunk).start()


def flag_columns(flags, step, blocks_step):
    shift = lax.rem(LANES - step * blocks_step, LANES)
    return pltpu.roll(flags, shift, 1).astype(BF16)


def chunk_at(step, chunk):
    return pl.ds(pl.multiple_of(step * chunk, chunk), chunk)


def normal_kernel(
    chunk,
    flags_hbm,
    snap_hbm,
    basis_hbm,
    out_ref,
    masked_hbm,
    flags_ref,
    basis_ref,
    snap_ref,
    masked_ref,
    gram_ref,
    right_ref,
    arrived,
    left,
    small,
):
    count, rows = snap_ref.shape
    modes = basis_ref.shape[0]
    half = modes // 2
    blocks_step = chunk // LANES
    steps = rows // chunk

    basis_copy = pltpu.make_async_copy(basis_hbm, basis_ref, small.at[0])
    flags_copy = pltpu.make_async_copy(flags_hbm, flags_ref, small.at[1])
    basis_copy.start()
    flags_copy.start()
    fetch_all(snap_hbm, snap_ref, arrived, chunk)
    right_ref[...] = jnp.zeros_like(right_ref)
    basis_copy.wait()
    flags_copy.wait()
    all_flags = flags_ref[...].astype(F32)

    for block in range(rows // LANES):
        piece = basis_ref[:, block * LANES : (block + 1) * LANES]
        copies = jnp.concatenate([piece] * (LANES // modes), axis=0)
        gram_ref[block * modes : (block + 1) * modes, :] = dot_nt(piece, copies)

    def body(step, carry):
        chunk_copy(snap_hbm, snap_ref, arrived, step, chunk).wait()
        columns = flag_columns(all_flags, step, blocks_step)
        here = chunk_at(step, chunk)
        source, target = snap_ref.at[:, here], masked_ref.at[:, here]
        for block in range(blocks_step):
            part = pl.ds(block * LANES, LANES)
            weight = jnp.broadcast_to(columns[:, block : block + 1], (count, LANES))
            target[:, part] = source[:, part] * weight
        chunk_copy(masked_ref, masked_hbm, left, step, chunk).start()
        right_ref[...] += dot_nt(target[...], basis_ref[:, here])
        return carry

    def drain(step, carry):
        chunk_copy(masked_ref, masked_hbm, left, step, chunk).wait()
        return carry

    lax.fori_loop(0, steps, body, 0)

    lane = lax.broadcasted_iota(jnp.int32, (LANES, LANES), 1)
    group = LANES // half
    tiles = []
    middle = jnp.zeros((LANES, LANES), F32)
    for tile_index in range(modes // group):
        tile = jnp.zeros((LANES, LANES), F32)
        for inner in range(group):
            mode = tile_index * group + inner
            entries = gram_ref[pl.ds(mode, LANES, stride=modes), :]
            moved = pltpu.roll(entries, (half * inner - mode) % LANES, 1)
            tile = jnp.where(lane // half == inner, moved, tile)
            if mode < half:
                middle = jnp.where(lane == mode + half, entries, middle)
        tiles.append(tile)
    tiles.append(middle)
    flags = flags_ref[...].astype(BF16)
    total = sum(
        dot_nn(flags, part) for part in split_three(jnp.concatenate(tiles, axis=1))
    )
    wide = LANES * (len(tiles) - 1)
    out_ref[:, :wide] = total[:, :wide]
    right = jnp.concatenate(
        [
            jnp.zeros((count, modes), F32),
            right_ref[...],
            jnp.zeros((count, LANES - 2 * modes), F32),
        ],
        axis=1,
    )
    out_ref[:, wide:] = total[:, wide:] + right
    lax.fori_loop(0, steps, drain, 0)


def normal_terms(flags, snapshots, basis, chunk=4096):
    count, rows = snapshots.shape
    modes = basis.shape[0]
    blocks = flags.shape[1]
    width = modes * modes // 2 + LANES
    hbm = pl.BlockSpec(memory_space=pl.ANY)
    return pl.pallas_call(
        functools.partial(normal_kernel, chunk),
        in_specs=[hbm] * 3,
        out_specs=[pl.BlockSpec(memory_space=pltpu.VMEM), hbm],
        out_shape=[
            jax.ShapeDtypeStruct((count, width), F32),
            jax.ShapeDtypeStruct((count, rows), BF16),
        ],
        scratch_shapes=[
            pltpu.VMEM((count, blocks), jnp.int32),
            pltpu.VMEM((modes, rows), BF16),
            pltpu.VMEM((count, rows), BF16),
            pltpu.VMEM((count, rows), BF16),
            pltpu.VMEM((blocks * modes, LANES), F32),
            pltpu.VMEM((count, modes), F32),
            pltpu.SemaphoreType.DMA((rows // chunk,)),
            pltpu.SemaphoreType.DMA((rows // chunk,)),
            pltpu.SemaphoreType.DMA((2,)),
        ],
        compiler_params=pltpu.CompilerParams(vmem_limit_bytes=SCRATCH_BYTES),
        name="normal_terms",
    )(
        pltpu.with_memory_space_constraint(flags, pltpu.HBM),
        snapshots,
        pltpu.with_memory_space_constraint(basis, pltpu.HBM),
    )


def solve_kernel(modes, shift, in_ref, out_ref, turned_ref, system_ref):
    half = modes // 2
    count, width = in_ref.shape
    padded = jnp.concatenate([in_ref[...], jnp.zeros((LANES - count, width), F32)], axis=0)
    turned_ref[...] = padded.T
    for mode in range(modes):
        first = min(half, modes - mode)
        base = mode * half
        start = mode * modes + mode
        values = turned_ref[base : base + first, :]
        system_ref[start : start + first, :] = values
        if first < half:
            wrapped = turned_ref[base + first : base + half, :]
            system_ref[pl.ds(mode, half - first, stride=modes), :] = wrapped
    middle = modes * half + half
    system_ref[pl.ds(half, half, stride=modes + 1), :] = turned_ref[middle : middle + half, :]
    right = turned_ref[modes * half + modes : modes * half + 2 * modes, :]
    index = lax.broadcasted_iota(jnp.int32, (modes, LANES), 0)

    rows = [system_ref[k * modes : (k + 1) * modes, :] for k in range(modes)]
    scaled = []
    targets = []
    for column in range(modes):
        row = jnp.where(index == column, rows[column] + shift, rows[column])
        inverse = 1.0 / row[column : column + 1, :]
        factor = jnp.where(index > column, row * inverse, 0.0)
        target = right[column : column + 1, :]
        scaled.append(factor)
        targets.append(target * inverse)
        right = right - factor * target
        for k in range(column + 1, modes):
            rows[k] = rows[k] - factor[k : k + 1, :] * row
    result = jnp.zeros((modes, LANES), F32)
    for column in reversed(range(modes)):
        value = targets[column] - jnp.sum(scaled[column] * result, axis=0, keepdims=True)
        result = jnp.where(index == column, value, result)
    square = jnp.concatenate([result, jnp.zeros((LANES - modes, LANES), F32)], axis=0)
    share = square.T[:count, :modes]
    high = out_ref.shape[1]
    dense = jnp.concatenate(
        [share[top : top + high, :] for top in range(0, count, high)], axis=1
    )
    for device in range(out_ref.shape[0]):
        out_ref[device] = dense


def solve_share(share, modes, rows_all, devices):
    count, width = share.shape
    return pl.pallas_call(
        functools.partial(solve_kernel, modes, DAMPING * rows_all),
        out_shape=jax.ShapeDtypeStruct((devices, count * modes // LANES, LANES), F32),
        scratch_shapes=[
            pltpu.VMEM((width, LANES), F32),
            pltpu.VMEM((modes * modes, LANES), F32),
        ],
        name="solve_share",
    )(share)


def packed_blocks(tiles):
    return [(i, (i + d) % tiles) for d in range(tiles // 2) for i in range(tiles)] + [
        (i, i + tiles // 2) for i in range(tiles // 2)
    ]


def refill_kernel(
    chunk,
    order,
    flags_ref,
    masked_hbm,
    basis_ref,
    shares_ref,
    fill_hbm,
    corr_ref,
    turned_ref,
    masked_ref,
    coef_ref,
    fill_ref,
    gap_ref,
    square_ref,
    sum_ref,
    arrived,
    left,
):
    count, rows = fill_ref.shape
    modes = basis_ref.shape[0]
    blocks = flags_ref.shape[1]
    group = square_ref.shape[1] // modes
    steps = rows // chunk
    side = count // 2
    fetch_all(masked_hbm, masked_ref, arrived, chunk)
    sum_ref[...] = jnp.zeros_like(sum_ref)
    square_ref[...] = jnp.zeros_like(square_ref)

    devices, high, _ = shares_ref.shape
    share_rows = count // devices
    for device in range(devices):
        dense = shares_ref[device]
        for place in range(share_rows // high):
            top = order[device] * share_rows + place * high
            coef_ref[top : top + high, :] = dense[:, place * modes : (place + 1) * modes]
    turned_ref[...] = coef_ref[...].T

    gaps = (1 - flags_ref[...]).astype(F32).astype(BF16)
    coef = coef_ref[...].astype(BF16).astype(F32)
    wide = jnp.concatenate([coef] * (2 * LANES // modes), axis=1)
    place = lax.broadcasted_iota(jnp.int32, (blocks, 2 * LANES), 0)
    owner = lax.broadcasted_iota(jnp.int32, (blocks, 2 * LANES), 1) // modes
    for part in range(blocks * modes // (2 * LANES)):
        first = part * (2 * LANES // modes)
        pick = jnp.where(place == owner + first, 1.0, 0.0).astype(BF16)
        gap_ref[:, part * 2 * LANES : (part + 1) * 2 * LANES] = (
            dot_nn(gaps, pick) * wide
        ).astype(BF16)

    def body(step, carry):
        here = chunk_at(step, chunk)
        chunk_copy(masked_hbm, masked_ref, arrived, step, chunk).wait()
        basis = basis_ref.at[:, here]
        masked, filled = masked_ref.at[:, here], fill_ref.at[:, here]
        weights = gap_ref.at[:, chunk_at(step, chunk // LANES * modes)]
        span = group * LANES
        for part in range(chunk // span):
            square = square_ref.at[part]
            for inner in range(group):
                square[
                    inner * modes : (inner + 1) * modes, inner * LANES : (inner + 1) * LANES
                ] = basis[:, part * span + inner * LANES : part * span + (inner + 1) * LANES]
            own = weights[:, part * group * modes : (part + 1) * group * modes]
            recon = dot_nn(own, square[...]).astype(BF16)
            lanes = pl.ds(part * span, span)
            filled[:, lanes] = masked[:, lanes] + recon
        chunk_copy(fill_ref, fill_hbm, left, step, chunk).start()
        upper, lower = filled[:side, :], filled[side:, :]
        sum_ref[:side, :side] += dot_nt(upper, upper)
        sum_ref[:side, side:] += dot_nt(upper, lower)
        sum_ref[side:, side:] += dot_nt(lower, lower)
        return carry

    def drain(step, carry):
        chunk_copy(fill_ref, fill_hbm, left, step, chunk).wait()
        return carry

    lax.fori_loop(0, steps, body, 0)
    for place, (i, j) in enumerate(packed_blocks(count // LANES)):
        i, j = min(i, j), max(i, j)
        corr_ref[place * LANES : (place + 1) * LANES, :] = sum_ref[
            i * LANES : (i + 1) * LANES, j * LANES : (j + 1) * LANES
        ]
    lax.fori_loop(0, steps, drain, 0)


def refill_correlate(flags, masked, basis, shares, order, chunk=4096, group=8):
    count, rows = masked.shape
    modes = basis.shape[0]
    packed = len(packed_blocks(count // LANES)) * LANES
    whole = pl.BlockSpec(memory_space=pltpu.VMEM)
    hbm = pl.BlockSpec(memory_space=pl.ANY)
    return pl.pallas_call(
        functools.partial(refill_kernel, chunk, order),
        in_specs=[whole, hbm, whole, whole],
        out_specs=[hbm, whole, whole],
        out_shape=[
            jax.ShapeDtypeStruct((count, rows), BF16),
            jax.ShapeDtypeStruct((packed, LANES), F32),
            jax.ShapeDtypeStruct((modes, count), F32),
        ],
        scratch_shapes=[
            pltpu.VMEM((count, rows), BF16),
            pltpu.VMEM((count, modes), F32),
            pltpu.VMEM((count, rows), BF16),
            pltpu.VMEM((count, flags.shape[1] * modes), BF16),
            pltpu.VMEM((chunk // (group * LANES), group * modes, group * LANES), BF16),
            pltpu.VMEM((count, count), F32),
            pltpu.SemaphoreType.DMA((rows // chunk,)),
            pltpu.SemaphoreType.DMA((rows // chunk,)),
        ],
        compiler_params=pltpu.CompilerParams(vmem_limit_bytes=SCRATCH_BYTES),
        name="refill_correlate",
    )(flags, masked, basis, shares)


def inverse_cholesky(products, panel=4):
    extent = products.shape[0]
    shape = (SUBLANES, 2 * extent)
    sub = lax.broadcasted_iota(jnp.int32, shape, 0)
    lane = lax.broadcasted_iota(jnp.int32, shape, 1)
    tiles = []
    for top in range(0, extent, SUBLANES):
        left = products[top : top + SUBLANES, :]
        both = jnp.concatenate([left, jnp.zeros_like(left)], axis=1)
        tiles.append(jnp.where(lane == sub + top + extent, 1.0, both))
    pivots = [jnp.ones(shape, F32) for _ in tiles]
    for start in range(0, extent, panel):
        first = start // SUBLANES
        inside = range(start, start + panel)
        spread = {
            (column, t): jnp.broadcast_to(tiles[t][:, column : column + 1], shape)
            for column in inside
            for t in range(first, len(tiles))
        }
        for column in inside:
            home, place = divmod(column, SUBLANES)
            pivot = spread[column, home][place : place + 1, :]
            inverse = 1.0 / pivot
            pivots[home] = jnp.where(sub == place, pivot, pivots[home])
            row = tiles[home][place : place + 1, :] * inverse
            later = range(column + 1, start + panel)
            values = {c: spread[c, home][place : place + 1, :] * inverse for c in later}
            for t in range(home, len(tiles)):
                factor = spread[column, t]
                if t == home:
                    factor = jnp.where(sub > place, factor, 0.0)
                for c in later:
                    spread[c, t] = spread[c, t] - factor * values[c]
                tiles[t] = tiles[t] - factor * row
    scaled = [tile / jnp.sqrt(pivot) for tile, pivot in zip(tiles, pivots)]
    return jnp.concatenate(scaled, axis=0)[:, extent:]


def sweep_weights(mixer, full, rows):
    spread = dot_nn(mixer, full, HIGHEST)
    products = dot_nt(spread, mixer, HIGHEST)
    return dot_nn(inverse_cholesky(products)[:rows], mixer, HIGHEST)


def first_kernel(bit_ref, mine_ref, other_ref, seed_ref, out_ref, full_ref):
    count = full_ref.shape[0]
    corr = joined(bit_ref, mine_ref, other_ref)
    for place, (i, j) in enumerate(packed_blocks(count // LANES)):
        i, j = min(i, j), max(i, j)
        tile = corr[place * LANES : (place + 1) * LANES, :]
        rows, cols = pl.ds(i * LANES, LANES), pl.ds(j * LANES, LANES)
        full_ref[rows, cols] = tile
        if i != j:
            full_ref[cols, rows] = tile.T
    mixer = seed_ref[...].astype(F32).T
    store_parts(out_ref, sweep_weights(mixer, full_ref[...], mixer.shape[0]))


def later_kernel(rows, scale, bit_ref, mine_ref, other_ref, full_ref, out_ref):
    mixer = joined(bit_ref, mine_ref, other_ref).astype(BF16).astype(F32)
    store_parts(out_ref, sweep_weights(mixer, full_ref[...], rows) * scale)


def store_parts(out_ref, values):
    rows = values.shape[0]
    for place, part in enumerate(split_three(values)):
        out_ref[place * rows : (place + 1) * rows, :] = part


def joined(bit_ref, mine_ref, other_ref):
    low = bit_ref[0] == 0
    mine, other = mine_ref[...], other_ref[...]
    return jnp.concatenate(
        [jnp.where(low, mine, other), jnp.where(low, other, mine)], axis=0
    )


def weight_specs(halves):
    scalar = pl.BlockSpec(memory_space=pltpu.SMEM)
    return [scalar] + [pl.BlockSpec(memory_space=pltpu.VMEM)] * halves


def first_weights(halves, seed):
    count, width = seed.shape
    return pl.pallas_call(
        first_kernel,
        in_specs=weight_specs(3),
        out_shape=[
            pltpu.VMEM((3 * width, count), BF16),
            pltpu.VMEM((count, count), F32),
        ],
        name="first_weights",
    )(*halves, seed)


def later_weights(halves, full, rows, scale):
    return pl.pallas_call(
        functools.partial(later_kernel, rows, scale),
        in_specs=weight_specs(3),
        out_shape=pltpu.VMEM((3 * rows, full.shape[0]), BF16),
        name="later_weights",
    )(*halves, full)


def mixer_kernel(chunk, weights_ref, fill_hbm, out_ref, fill_ref, sum_ref, arrived):
    width = out_ref.shape[0]
    fetch_all(fill_hbm, fill_ref, arrived, chunk)
    sum_ref[...] = jnp.zeros_like(sum_ref)

    def body(step, carry):
        chunk_copy(fill_hbm, fill_ref, arrived, step, chunk).wait()
        filled = fill_ref[:, chunk_at(step, chunk)]
        terms = dot_nn(weights_ref[...], filled)
        ortho = terms[:width] + (terms[width : 2 * width] + terms[2 * width :])
        sum_ref[...] += dot_nt(filled, ortho.astype(BF16))
        return carry

    lax.fori_loop(0, fill_ref.shape[1] // chunk, body, 0)
    out_ref[...] = sum_ref[...].T


def next_mixer(weights, filled, chunk=4096):
    count, rows = filled.shape
    width = weights.shape[0] // 3
    whole = pl.BlockSpec(memory_space=pltpu.VMEM)
    return pl.pallas_call(
        functools.partial(mixer_kernel, chunk),
        in_specs=[whole, pl.BlockSpec(memory_space=pl.ANY)],
        out_specs=whole,
        out_shape=jax.ShapeDtypeStruct((width, count), F32),
        scratch_shapes=[
            pltpu.VMEM((count, rows), BF16),
            pltpu.VMEM((count, width), F32),
            pltpu.SemaphoreType.DMA((rows // chunk,)),
        ],
        compiler_params=pltpu.CompilerParams(vmem_limit_bytes=SCRATCH_BYTES),
        name="next_mixer",
    )(weights, filled)


def basis_kernel(chunk, weights_ref, fill_hbm, out_hbm, fill_ref, out_ref, arrived, left):
    modes, rows = out_ref.shape
    fetch_all(fill_hbm, fill_ref, arrived, chunk)

    def body(step, carry):
        here = chunk_at(step, chunk)
        chunk_copy(fill_hbm, fill_ref, arrived, step, chunk).wait()
        terms = dot_nn(weights_ref[...], fill_ref[:, here])
        out_ref[:, here] = terms[:modes] + (terms[modes : 2 * modes] + terms[2 * modes :])
        chunk_copy(out_ref, out_hbm, left, step, chunk).start()
        return carry

    def drain(step, carry):
        chunk_copy(out_ref, out_hbm, left, step, chunk).wait()
        return carry

    lax.fori_loop(0, rows // chunk, body, 0)
    lax.fori_loop(0, rows // chunk, drain, 0)


def project_basis(weights, filled, chunk=4096):
    count, rows = filled.shape
    modes = weights.shape[0] // 3
    hbm = pl.BlockSpec(memory_space=pl.ANY)
    return pl.pallas_call(
        functools.partial(basis_kernel, chunk),
        in_specs=[pl.BlockSpec(memory_space=pltpu.VMEM), hbm],
        out_specs=hbm,
        out_shape=jax.ShapeDtypeStruct((modes, rows), F32),
        scratch_shapes=[
            pltpu.VMEM((count, rows), BF16),
            pltpu.VMEM((modes, rows), F32),
            pltpu.SemaphoreType.DMA((rows // chunk,)),
            pltpu.SemaphoreType.DMA((rows // chunk,)),
        ],
        compiler_params=pltpu.CompilerParams(vmem_limit_bytes=SCRATCH_BYTES),
        name="project_basis",
    )(weights, filled)


class Stage:
    def __init__(self, axis, size, bits):
        self.axis = axis
        self.pairs = [(i, i ^ (1 << bits[i & 1])) for i in range(size)]
        self.bits = bits

    def bit(self):
        place = lax.axis_index(self.axis)
        if self.bits[0] == self.bits[1]:
            return (place >> self.bits[0]) & 1
        return jnp.where(place & 1, place >> self.bits[1], place >> self.bits[0]) & 1

    def swap(self, values):
        return lax.ppermute(values, self.axis, self.pairs)


def stages():
    rows, sub = (lax.axis_size(name) for name in AXES)
    high = list(range(1, rows.bit_length() - 1))
    plan = [Stage("rows", rows, (0, 0))]
    plan += [Stage("rows", rows, bits) for bits in zip(high, reversed(high))]
    plan += [Stage("sub", sub, (bit, bit)) for bit in range(sub.bit_length() - 1)]
    return plan


def halve(values, stage):
    bit = stage.bit()
    half = values.shape[0] // 2
    keep = lax.dynamic_slice_in_dim(values, bit * half, half, 0)
    send = lax.dynamic_slice_in_dim(values, (1 - bit) * half, half, 0)
    return keep + stage.swap(send)


def join(values, stage):
    other = stage.swap(values)
    low = stage.bit() == 0
    return jnp.concatenate(
        [jnp.where(low, values, other), jnp.where(low, other, values)], axis=0
    )


def scatter_sum(values):
    for stage in stages():
        values = halve(values, stage)
    return values


def share_order():
    rows, sub = (lax.axis_size(name) for name in AXES)
    order = []
    for row in range(rows):
        for column in range(sub):
            place = 0
            for stage in stages():
                index = row if stage.axis == "rows" else column
                place = 2 * place + ((index >> stage.bits[row & 1]) & 1)
            order.append(place)
    return order


def sum_everywhere(values, halvings):
    plan = stages()
    for stage in plan[:halvings]:
        values = halve(values, stage)
    for stage in plan[halvings:]:
        values = values + stage.swap(values)
    for stage in reversed(plan[1:halvings]):
        values = join(values, stage)
    core = plan[0]
    return core.bit().astype(jnp.int32).reshape(1), values, core.swap(values)


def per_device(old_basis, snapshots, gap_flags, sketch_seed):
    modes = old_basis.shape[0]
    rows_all = old_basis.shape[1] * lax.axis_size(AXES)
    terms, masked = normal_terms(gap_flags, snapshots, old_basis)
    devices = lax.axis_size(AXES)
    shares = solve_share(scatter_sum(terms), modes, rows_all, devices)
    shares = lax.all_to_all(shares, AXES, 0, 0, tiled=True)
    filled, corr, coefs = refill_correlate(gap_flags, masked, old_basis, shares, share_order())
    weights, full = first_weights(sum_everywhere(corr, 2), sketch_seed)
    width = sketch_seed.shape[1]
    for sweep in range(1, POWER + 1):
        halves = sum_everywhere(next_mixer(weights, filled), 1)
        if sweep < POWER:
            weights = later_weights(halves, full, width, 1.0)
        else:
            weights = later_weights(halves, full, modes, math.sqrt(rows_all))
    return project_basis(weights, filled), coefs


def solution(mesh):
    split = P(None, AXES)
    return jax.shard_map(
        per_device,
        mesh=mesh,
        in_specs=(split, split, split, P()),
        out_specs=(split, P()),
        check_vma=False,
    )
```
